32 devices in a mesh: groups: 2 (over x), ctx: 16 (over z, y, core).
Axes of the slice: x: 2, y: 2, z: 4, core: 2. Of those that a mesh axis runs over, the one named last changes fastest.
Arguments:
- queries: bfloat16 [4096, 4096], P(('groups', 'ctx')), parts along dimension 0, may hold values from -12 to 12
- keys: bfloat16 [4096, 512], P(('groups', 'ctx')), parts along dimension 0, may hold values from -9 to 9
- values: bfloat16 [4096, 512], P(('groups', 'ctx')), parts along dimension 0, may hold values from -6 to 6
- doc_lengths: int32 [32], P('groups'), parts along dimension 0, may hold values from 1 to 1024, 2048 in all
Outputs:
- attended: bfloat16 [4096, 4096], P(('groups', 'ctx')), parts along dimension 0
The draws below stay inside these ranges and needn't reach their ends.
There are 2 independent parts, one for each index of `groups`. The reference program is written for one: setup_inputs(seed, part) draws one part's arguments, and reference() takes and returns one part's arrays. A program takes and returns all parts, laid end to end along the dimension named above; each array names one. Nothing has to cross between parts.
Inputs may be any that keep to these rules, and one draw needn't show every extreme that they name: `doc_lengths`: the lengths sum to 2048, and the longest document has exactly 1024 tokens.
All inputs are finite; a program needn't handle non-finite values.
Results may differ from the reference program's by a relative error of at most 0.003.
Values may be sent and summed in bfloat16 or wider, within the bound.
A program may use at most 128 MiB of HBM per device.

```python
import math
import jax
import jax.numpy as jnp
import numpy as np
from jax import lax

HEADS = 32
KV_HEADS = 4
HEAD_DIM = 128
NDOC = 16
WINDOW_TOKENS = 2048


def draw_queries(key, part):
    drawn_values = jax.random.normal(jax.random.fold_in(key, 11), (WINDOW_TOKENS, HEADS, HEAD_DIM), jnp.float32) * 2.0
    drawn_values = jnp.clip(drawn_values, -12.0, 12.0)
    return drawn_values.reshape(WINDOW_TOKENS, HEADS * HEAD_DIM).astype(jnp.bfloat16)


def draw_keys(key, part):
    drawn_values = jax.random.normal(jax.random.fold_in(key, 12), (WINDOW_TOKENS, KV_HEADS, HEAD_DIM), jnp.float32) * 1.5
    drawn_values = jnp.clip(drawn_values, -9.0, 9.0)
    return drawn_values.reshape(WINDOW_TOKENS, KV_HEADS * HEAD_DIM).astype(jnp.bfloat16)


def shard_levels(key, extent, pieces, smallest, largest):
    factor_of = 1.0
    for dim, shards_of in pieces:
        draws = jax.random.uniform(jax.random.fold_in(jax.random.fold_in(key, 6), dim), (shards_of,), jnp.float32, smallest / len(pieces), largest / len(pieces))
        factor_of = factor_of * jnp.repeat(jnp.exp(draws), extent[dim] // shards_of).reshape((-1,) + (1,) * (len(extent) - 1 - dim))
    return factor_of


def profile(amount, total, limit, slope):
    loads = [(1 << 20) // math.isqrt(grade ** slope) + 1 for grade in range(2, amount + 1)]
    spare, counts = total - limit - (amount - 1), [1] * (amount - 1)
    while spare > 0:
        free = [i for i in range(amount - 1) if counts[i] < limit]
        whole, budget = sum([loads[i] for i in free]), spare
        for i in free:
            addition = min(limit - counts[i], max(1, budget * loads[i] // whole), spare)
            counts[i] = counts[i] + addition
            spare = spare - addition
    return np.array([limit] + counts)


def ragged_sizes(key, number_of, total, limit, lean):
    if number_of == 2:
        one = jax.random.randint(key, (), max(1, total - limit), min(limit, total - 1) + 1)
        return jnp.stack([one, total - one])
    tallies = jnp.asarray(profile(number_of, total, limit, lean), jnp.int32)
    pairs = (number_of - 1) // 2
    giver, taker = tallies[1:1 + 2 * pairs:2], tallies[2:2 + 2 * pairs:2]
    slack = jnp.minimum(giver - 1, limit - taker)
    passed = jax.random.randint(jax.random.fold_in(key, 1), (pairs,), 0, 1 << 20) % (slack + 1)
    tallies = tallies.at[1:1 + 2 * pairs:2].set(giver - passed).at[2:2 + 2 * pairs:2].set(taker + passed)
    return tallies[jax.random.permutation(jax.random.fold_in(key, 2), number_of)]


def scatter_about(own_key, dims, scale, limit, cuts=(), kind=jnp.bfloat16):
    values = jax.random.normal(own_key, dims, jnp.float32) * scale
    if len(cuts) > 0:
        values = shard_levels(own_key, dims, cuts, -0.22, 0.18) * values
    return jnp.clip(values, min=-limit, max=limit).astype(kind)


def setup_inputs(seed: int = 0, part: int = 0) -> dict:
    key_list = jax.random.split(jax.random.key(seed), 5)
    part_splits = jax.random.split(jax.random.fold_in(key_list[4], part), 5)
    queries = draw_queries(jax.random.fold_in(jax.random.fold_in(key_list[4], part), 71), part)
    keys = draw_keys(jax.random.fold_in(jax.random.fold_in(key_list[4], part), 71), part)
    values = scatter_about(part_splits[2], (WINDOW_TOKENS, KV_HEADS * HEAD_DIM), 1.0, 6.0, ((0, 16),))
    doc_lengths = ragged_sizes(part_splits[3], NDOC, WINDOW_TOKENS, WINDOW_TOKENS // 2, 2).astype(jnp.int32)
    return dict(queries=queries, keys=keys, values=values, doc_lengths=doc_lengths)


negative_filler = -1e+30

def doc_index(positions, doc_ends):
    return lax.optimization_barrier(jnp.sum((doc_ends[None, :] <= positions[:, None]).astype(jnp.int32), axis=1))

def reference(queries, keys, values, doc_lengths):
    group_size = HEADS // KV_HEADS
    doc_ends = jnp.cumsum(doc_lengths).astype(jnp.int32)
    positions = jnp.arange(WINDOW_TOKENS, dtype=jnp.int32)
    doc_ids = doc_index(positions, doc_ends)
    key_wide = keys.reshape(WINDOW_TOKENS, KV_HEADS, HEAD_DIM).astype(jnp.float32)
    value_wide = values.reshape(WINDOW_TOKENS, KV_HEADS, HEAD_DIM).astype(jnp.float32)
    block_rows = math.gcd(WINDOW_TOKENS, 128)
    scale_factor = 1.0 / math.sqrt(HEAD_DIM)

    def single_block(block_start):
        query_block = lax.dynamic_slice_in_dim(queries, block_start, block_rows, 0)
        query_block = query_block.reshape(block_rows, KV_HEADS, group_size, HEAD_DIM).astype(jnp.float32)
        query_position = block_start + jnp.arange(block_rows, dtype=jnp.int32)
        query_doc = lax.dynamic_slice_in_dim(doc_ids, block_start, block_rows, 0)
        visible = (doc_ids[None, :] == query_doc[:, None]) & (positions[None, :] <= query_position[:, None])
        logit_scores = jnp.einsum('qhgd,khd->hgqk', query_block, key_wide) * scale_factor
        logit_scores = jnp.where(visible[None, None], logit_scores, negative_filler)
        row_max = lax.optimization_barrier(jnp.max(logit_scores, axis=3, keepdims=True))
        attention_weight = jnp.where(visible[None, None], jnp.exp(logit_scores - row_max), 0.0)
        denominator = lax.optimization_barrier(jnp.sum(attention_weight, axis=3))
        rounded = lax.optimization_barrier(attention_weight.astype(jnp.bfloat16)).astype(jnp.float32)
        summed = jnp.einsum('hgqk,khd->qhgd', rounded, value_wide)
        result = summed / jnp.transpose(denominator, (2, 0, 1))[..., None]
        return result.reshape(block_rows, HEADS * HEAD_DIM).astype(jnp.bfloat16)
    block_starts = jnp.arange(WINDOW_TOKENS // block_rows, dtype=jnp.int32) * block_rows
    blocks = lax.map(single_block, block_starts)
    return blocks.reshape(WINDOW_TOKENS, HEADS * HEAD_DIM)
```

```python
import functools
import math

import jax
import jax.numpy as jnp
from jax import lax
from jax.experimental import pallas as pl
from jax.experimental.pallas import tpu as pltpu
from jax.sharding import PartitionSpec as P

HEADS = 32
KV_HEADS = 4
HEAD_DIM = 128
GROUP = HEADS // KV_HEADS
FILLER = -1e30
MAIN_HEADS = 2
TAIL_HEADS = 4
ORDER = (
    ("relay", 0),
    ("relay", 1),
    ("main", (0,)),
    ("relay", 2),
    ("main", (1,)),
    ("relay", 3),
    ("main", (2,)),
    ("last", 0),
    ("main", (3,)),
    ("last", 1),
    ("tail", (0,)),
    ("last", 2),
    ("tail", (1,)),
    ("last", 3),
    ("tail", (2,)),
    ("tail", (3,)),
)


def kernel(
    n, level, q_hbm, k_hbm, v_hbm, len_hbm, out_ref,
    q_buf, kv_buf, bias, len_buf, part_sum, part_top,
    own_sem, q_sem, len_sem, send_sem, recv_sem,
):
    rows = q_hbm.shape[0]
    reach = n // 2
    far = reach // level
    planes = n // level
    width = (reach + 1) * rows
    me = lax.axis_index("ctx")
    z, r = me // level, me % level
    core = r + 1 - 2 * (r % 2)
    side = (r + 2) % level
    side_core = core + side - r

    def slot(d, lane):
        return (far - d) * level + lane

    def part(j, s):
        return kv_buf.at[j, :, pl.ds(pl.multiple_of(s * rows, rows), rows), :]

    def move(j, s, s_there, kind, device):
        return pltpu.make_async_remote_copy(
            src_ref=part(j, s), dst_ref=part(j, s_there),
            send_sem=send_sem.at[j, s, kind], recv_sem=recv_sem.at[j, s_there],
            device_id={"ctx": device}, device_id_type=pl.DeviceIdType.MESH,
        )

    def need(d, source, target):
        distance = d * level + target - source
        return (distance >= 0) & (distance <= reach)

    def there(d):
        return z >= d

    sent = []

    def send(condition, j, s, s_there, kind, device):
        @pl.when(condition)
        def _():
            move(j, s, s_there, kind, device).start()

        sent.append((condition, j, s, s_there, kind, device))

    def arrived(condition, j, s):
        @pl.when(condition)
        def _():
            move(j, s, s, 0, me - r + core).wait_recv()

    barrier = pltpu.get_barrier_semaphore()

    def greet(device):
        pl.semaphore_signal(
            barrier, inc=1, device_id={"ctx": device}, device_id_type=pl.DeviceIdType.MESH
        )

    greet(me - r + core)
    if level > 2:
        greet(me - r + side)

    @pl.when(z > 0)
    def _():
        greet(me - level)

    @pl.when(z < planes - 1)
    def _():
        greet(me + level)

    own = slot(0, r)
    own_copies = []
    for j in range(KV_HEADS):
        for t, ref in enumerate((k_hbm, v_hbm)):
            own_copies.append(pltpu.make_async_copy(
                ref.at[:, pl.ds(j * HEAD_DIM, HEAD_DIM)],
                kv_buf.at[j, t, pl.ds(pl.multiple_of(own * rows, rows), rows), :],
                own_sem.at[j, t],
            ))
            own_copies[-1].start()
    q_copy = pltpu.make_async_copy(q_hbm, q_buf, q_sem)
    q_copy.start()
    len_copy = pltpu.make_async_copy(len_hbm, len_buf, len_sem)
    len_copy.start()

    pl.semaphore_wait(
        barrier,
        (2 if level > 2 else 1) + (z > 0).astype(jnp.int32) + (z < planes - 1).astype(jnp.int32),
    )

    def spread(d, j):
        s = slot(d, r)
        if d < far:
            send(there(d) & (z < planes - 1), j, s, slot(d + 1, r), 0, me + level)
        if level > 2:
            send(
                there(d) & (need(d, r, side) | need(d, r, side_core)),
                j, s, s, 1, me - r + side,
            )
        send(there(d) & need(d, r, core), j, s, s, 2, me - r + core)

    def from_plane(j, d):
        arrived(there(d), j, slot(d, r))
        spread(d, j)

    def from_side(j, d):
        if level > 2:
            s = slot(d, side)
            wanted = there(d) & (need(d, side, r) | need(d, side, core))
            arrived(wanted, j, s)
            send(there(d) & need(d, side, core), j, s, s, 2, me - r + core)

    def from_core(j, d):
        arrived(there(d) & need(d, core, r), j, slot(d, core))

    def from_core_side(j, d):
        if level > 2:
            arrived(there(d) & need(d, side_core, r), j, slot(d, side_core))

    unit = (
        lax.broadcasted_iota(jnp.int32, (rows, rows), 0)
        == lax.broadcasted_iota(jnp.int32, (rows, rows), 1)
    ).astype(bias.dtype)
    factor = math.log2(math.e) / math.sqrt(HEAD_DIM)

    def blocks(pieces):
        return [pl.ds(pl.multiple_of(first * rows, rows), count * rows) for first, count in pieces]

    main_pieces = [(level, reach + 1 - level)]
    tail_pieces = [(0, level)]

    def operands(j, pieces):
        places = blocks([(r + first, count) for first, count in pieces])
        keys = jnp.concatenate([kv_buf[j, 0, p, :] for p in places], axis=0)
        mask = jnp.concatenate([bias[p, :] for p in blocks(pieces)], axis=0)
        value_block = jnp.concatenate([kv_buf[j, 1, p, :] for p in places], axis=0)
        wide = jnp.concatenate([value_block, jnp.ones_like(value_block)], axis=1)
        return jnp.concatenate([keys, mask], axis=1), wide

    def columns(j, step, heads):
        first = j * GROUP + step * heads
        return [pl.ds((first + h) * HEAD_DIM, HEAD_DIM) for h in range(heads)]

    def pipelined(chosen, pieces, heads, ahead, finish):
        tasks = [(j, step) for j in chosen for step in range(GROUP // heads)]
        queue = []

        def begin(j, step):
            block = jnp.concatenate(
                [jnp.concatenate([q_buf[:, c], unit], axis=1) for c in columns(j, step, heads)],
                axis=0,
            )
            key_block, wide = operands(j, pieces)
            queue.append((lax.dot_general(
                block, key_block, (((1,), (1,)), ((), ())), preferred_element_type=jnp.float32
            ), wide))

        for task in tasks[:ahead]:
            begin(*task)
        for i, (j, step) in enumerate(tasks):
            if i + ahead < len(tasks):
                begin(*tasks[i + ahead])
            finish(j, step, heads, *queue.pop(0))

    def main_finish(j, step, heads, scores, wide):
        part = pl.ds(step * heads * rows, heads * rows)
        top = jnp.max(scores, axis=1, keepdims=True)
        weights = jnp.exp2((scores - top) * factor).astype(jnp.bfloat16)
        part_sum[j, part, :] = jnp.dot(weights, wide, preferred_element_type=jnp.float32)
        part_top[j, part, :] = jnp.broadcast_to(top, (heads * rows, HEAD_DIM))

    def tail_finish(j, step, heads, scores, wide):
        part = pl.ds(step * heads * rows, heads * rows)
        before = part_top[j, part, :]
        top = jnp.maximum(before, jnp.max(scores, axis=1, keepdims=True))
        weights = jnp.exp2((scores - top[:, :1]) * factor).astype(jnp.bfloat16)
        kept = jnp.exp2((before - top) * factor)
        total = jnp.dot(weights, wide, preferred_element_type=jnp.float32)
        summed = total[:, :HEAD_DIM] + kept * part_sum[j, part, :HEAD_DIM]
        weight = total[:, HEAD_DIM:] + kept * part_sum[j, part, HEAD_DIM:]
        result = (summed / weight).astype(out_ref.dtype)
        for h, c in enumerate(columns(j, step, heads)):
            out_ref[:, c] = result[h * rows:(h + 1) * rows]

    def stage(kind, what):
        if kind == "relay":
            from_side(what, far - 1)
            from_plane(what, far)
        elif kind == "last":
            from_side(what, far)
        elif kind == "main":
            for j in what:
                for d in range(far):
                    from_core(j, d)
                    from_core_side(j, d)
            pipelined(what, main_pieces, MAIN_HEADS, 2, main_finish)
        else:
            for j in what:
                from_core(j, far)
                from_core_side(j, far)
            pipelined(what, tail_pieces, TAIL_HEADS, 1, tail_finish)

    for j in range(KV_HEADS):
        own_copies[2 * j].wait()
        own_copies[2 * j + 1].wait()
        spread(0, j)

    for d in range(1, far + 1):
        @pl.when(z < d)
        def _():
            @pl.loop(0, KV_HEADS)
            def _(j):
                kv_buf[j, :, pl.ds(slot(d, 0) * rows, level * rows), :] = jnp.zeros(
                    (2, level * rows, HEAD_DIM), kv_buf.dtype
                )

    len_copy.wait()
    position = me * rows + lax.broadcasted_iota(jnp.int32, (1, rows), 1)
    start = jnp.zeros((1, rows), jnp.int32)
    end = jnp.int32(0)
    for k in range(len_buf.shape[0]):
        end = end + len_buf[k]
        start = jnp.where(end <= position, end, start)
    key_position = (me - reach) * rows + lax.broadcasted_iota(jnp.int32, (width, rows), 0)
    visible = (key_position >= start) & (key_position <= position)
    bias[...] = jnp.where(visible, 0.0, FILLER).astype(bias.dtype)

    for d in range(1, far):
        for j in range(KV_HEADS):
            from_plane(j, d)
            from_side(j, d - 1)
    q_copy.wait()
    for kind, what in ORDER:
        stage(kind, what)

    for condition, *rest in sent:
        @pl.when(condition)
        def _():
            move(*rest).wait_send()


def solution(mesh):
    n = mesh.shape["ctx"]
    level = max(2, 8 // mesh.shape["groups"])

    def local(queries, keys, values, doc_lengths):
        rows = queries.shape[0]
        reach = n // 2
        slots = reach + level
        return pl.pallas_call(
            functools.partial(kernel, n, level),
            out_shape=jax.ShapeDtypeStruct(queries.shape, queries.dtype),
            in_specs=[pl.BlockSpec(memory_space=pltpu.HBM)] * 4,
            out_specs=pl.BlockSpec(memory_space=pltpu.VMEM),
            scratch_shapes=[
                pltpu.VMEM(queries.shape, queries.dtype),
                pltpu.VMEM((KV_HEADS, 2, slots * rows, HEAD_DIM), keys.dtype),
                pltpu.VMEM(((reach + 1) * rows, rows), keys.dtype),
                pltpu.SMEM(doc_lengths.shape, doc_lengths.dtype),
                pltpu.VMEM((KV_HEADS, GROUP * rows, 2 * HEAD_DIM), jnp.float32),
                pltpu.VMEM((KV_HEADS, GROUP * rows, HEAD_DIM), jnp.float32),
                pltpu.SemaphoreType.DMA((KV_HEADS, 2)),
                pltpu.SemaphoreType.DMA,
                pltpu.SemaphoreType.DMA,
                pltpu.SemaphoreType.DMA((KV_HEADS, slots, 3)),
                pltpu.SemaphoreType.DMA((KV_HEADS, slots)),
            ],
            compiler_params=pltpu.CompilerParams(collective_id=0, has_side_effects=True,
                                                 vmem_limit_bytes=min(60 << 20, (3 * n // 2 + 8) << 20)),
        )(*(
            pltpu.with_memory_space_constraint(x, pltpu.HBM)
            for x in (queries, keys, values, doc_lengths)
        ))

    spec = P(("groups", "ctx"), None)
    return jax.shard_map(
        local, mesh=mesh, in_specs=(spec, spec, spec, P("groups")), out_specs=spec, check_vma=False
    )
```

```python
import functools
import math

import jax
import jax.numpy as jnp
from jax import lax
from jax.experimental import pallas as pl
from jax.experimental.pallas import tpu as pltpu
from jax.sharding import PartitionSpec as P

HEADS = 32
KV_HEADS = 4
HEAD_DIM = 128
GROUP = HEADS // KV_HEADS
FILLER = -1e30
BY_PLANE = 1
MAIN_HEADS = 2
MAIN_AHEAD = 2
MIDDLE_HEADS = 2
MIDDLE_AHEAD = 0
TAIL_HEADS = 2
TAIL_AHEAD = 0
ORDER = (
    ("near", 0),
    ("near", 1),
    ("main", 0),
    ("near", 2),
    ("main", 1),
    ("near", 3),
    ("main", 2),
    ("relay", 0),
    ("main", 3),
    ("relay", 1),
    ("middle", 0),
    ("relay", 2),
    ("middle", 1),
    ("relay", 3),
    ("middle", 2),
    ("last", 0),
    ("middle", 3),
    ("last", 1),
    ("last", 3),
    ("tail", 0),
    ("last", 2),
    ("tail", 1),
    ("tail", 3),
    ("tail", 2),
)


def kernel(
    n, level, q_hbm, k_hbm, v_hbm, len_hbm, out_ref,
    q_buf, kv_buf, bias, len_buf, part_sum, part_top,
    own_sem, q_sem, len_sem, send_sem, recv_sem,
):
    rows = q_hbm.shape[0]
    reach = n // 2
    far = reach // level
    planes = n // level
    me = lax.axis_index("ctx")
    z, r = me // level, me % level
    core = r + 1 - 2 * (r % 2)
    side = (r + 2) % level
    side_core = core + side - r

    def slot(d, lane):
        return (far - d) * level + lane

    def part(j, s):
        return kv_buf.at[j, :, pl.ds(pl.multiple_of(s * rows, rows), rows), :]

    def move(j, s, s_there, kind, device):
        return pltpu.make_async_remote_copy(
            src_ref=part(j, s), dst_ref=part(j, s_there),
            send_sem=send_sem.at[j, s, kind], recv_sem=recv_sem.at[j, s_there],
            device_id={"ctx": device}, device_id_type=pl.DeviceIdType.MESH,
        )

    def need(d, source, target):
        distance = d * level + target - source
        return (distance >= 0) & (distance <= reach)

    def there(d):
        return z >= d

    sent = []

    def send(condition, j, s, s_there, kind, device):
        @pl.when(condition)
        def _():
            move(j, s, s_there, kind, device).start()

        sent.append((condition, j, s, s_there, kind, device))

    def arrived(condition, j, s):
        @pl.when(condition)
        def _():
            move(j, s, s, 0, me - r + core).wait_recv()

    barrier = pltpu.get_barrier_semaphore()

    def greet(device):
        pl.semaphore_signal(
            barrier, inc=1, device_id={"ctx": device}, device_id_type=pl.DeviceIdType.MESH
        )

    greet(me - r + core)
    if level > 2:
        greet(me - r + side)

    @pl.when(z > 0)
    def _():
        greet(me - level)

    @pl.when(z < planes - 1)
    def _():
        greet(me + level)

    own = slot(0, r)
    own_copies = []
    for j in range(KV_HEADS):
        for t, ref in enumerate((k_hbm, v_hbm)):
            own_copies.append(pltpu.make_async_copy(
                ref.at[:, pl.ds(j * HEAD_DIM, HEAD_DIM)],
                kv_buf.at[j, t, pl.ds(pl.multiple_of(own * rows, rows), rows), :],
                own_sem.at[j, t],
            ))
            own_copies[-1].start()
    q_copy = pltpu.make_async_copy(q_hbm, q_buf, q_sem)
    q_copy.start()
    len_copy = pltpu.make_async_copy(len_hbm, len_buf, len_sem)
    len_copy.start()

    pl.semaphore_wait(
        barrier,
        (2 if level > 2 else 1) + (z > 0).astype(jnp.int32) + (z < planes - 1).astype(jnp.int32),
    )

    def by_plane(j):
        return level > 2 and j >= KV_HEADS - BY_PLANE

    def spread(d, j):
        s = slot(d, r)
        if d < far:
            send(there(d) & (z < planes - 1), j, s, slot(d + 1, r), 0, me + level)
        if level > 2 and not (d == far and by_plane(j)):
            send(
                there(d) & (need(d, r, side) | need(d, r, side_core)),
                j, s, s, 1, me - r + side,
            )
        send(there(d) & need(d, r, core), j, s, s, 2, me - r + core)

    def from_plane(j, d):
        arrived(there(d), j, slot(d, r))
        spread(d, j)

    def from_side(j, d):
        if level > 2:
            s = slot(d, side)
            wanted = there(d) & (need(d, side, r) | need(d, side, core))
            if by_plane(j) and d == far:
                wanted = there(d) & (r < level // 2)
            arrived(wanted, j, s)
            if by_plane(j) and d == far - 1:
                climbs = there(d) & (r < level // 2) & (z < planes - 1)
                send(climbs, j, s, slot(far, side), 0, me + level)
            send(there(d) & need(d, side, core), j, s, s, 2, me - r + core)

    def from_core(j, d):
        arrived(there(d) & need(d, core, r), j, slot(d, core))

    def from_core_side(j, d):
        if level > 2:
            arrived(there(d) & need(d, side_core, r), j, slot(d, side_core))

    unit = (
        lax.broadcasted_iota(jnp.int32, (rows, rows), 0)
        == lax.broadcasted_iota(jnp.int32, (rows, rows), 1)
    ).astype(bias.dtype)
    factor = math.log2(math.e) / math.sqrt(HEAD_DIM)

    def blocks(pieces):
        return [pl.ds(pl.multiple_of(first * rows, rows), count * rows) for first, count in pieces]

    if level > 2:
        upper = r // 2
        third = (r == 2).astype(jnp.int32)
        first = (r == 0).astype(jnp.int32)
        main_pieces = [
            (4 + upper * (r + 1), 4 + upper * (r + 1) - r, 2),
            (8 + upper * (r - 1), 8 + upper * (r - 1) - r, 1),
            (8 + r, 8 + first, 1),
        ]
        middle_pieces = [
            (r + 2 * upper, 2 * upper, 1),
            (7 - third - 6 * first, 9 - 8 * first, 1),
            (6 - third, 6 - third - r, 2),
        ]
        tail_pieces = [(2 + r // 3, 2 + r // 3 - r, 2)]
    else:
        main_pieces = [(r + level, level, reach + 1 - level)]
        tail_pieces = [(r, 0, level)]

    def operands(j, pieces):
        places = blocks([(place, count) for place, _, count in pieces])
        keys = jnp.concatenate([kv_buf[j, 0, p, :] for p in places], axis=0)
        mask = jnp.concatenate(
            [bias[p, :] for p in blocks([(distance, count) for _, distance, count in pieces])], axis=0
        )
        value_block = jnp.concatenate([kv_buf[j, 1, p, :] for p in places], axis=0)
        wide = jnp.concatenate([value_block, jnp.ones_like(value_block)], axis=1)
        return jnp.concatenate([keys, mask], axis=1), wide

    def columns(j, step, heads):
        first = j * GROUP + step * heads
        return [pl.ds((first + h) * HEAD_DIM, HEAD_DIM) for h in range(heads)]

    def pipelined(chosen, pieces, heads, ahead, finish):
        tasks = [(j, step) for j in chosen for step in range(GROUP // heads)]
        queue = []

        def begin(j, step):
            block = jnp.concatenate(
                [jnp.concatenate([q_buf[:, c], unit], axis=1) for c in columns(j, step, heads)],
                axis=0,
            )
            key_block, wide = operands(j, pieces)
            queue.append((lax.dot_general(
                block, key_block, (((1,), (1,)), ((), ())), preferred_element_type=jnp.float32
            ), wide))

        for task in tasks[:ahead]:
            begin(*task)
        for i, (j, step) in enumerate(tasks):
            if i + ahead < len(tasks):
                begin(*tasks[i + ahead])
            finish(j, step, heads, *queue.pop(0))

    def main_finish(j, step, heads, scores, wide):
        part = pl.ds(step * heads * rows, heads * rows)
        top = jnp.max(scores, axis=1, keepdims=True)
        weights = jnp.exp2((scores - top) * factor).astype(jnp.bfloat16)
        part_sum[j, part, :] = jnp.dot(weights, wide, preferred_element_type=jnp.float32)
        part_top[j, part, :] = jnp.broadcast_to(top, (heads * rows, HEAD_DIM))

    def joined(j, part, scores, wide):
        before = part_top[j, part, :]
        top = jnp.maximum(before, jnp.max(scores, axis=1, keepdims=True))
        spread_top = jnp.concatenate([top] * (scores.shape[1] // HEAD_DIM), axis=1)
        weights = jnp.exp2((scores - spread_top) * factor).astype(jnp.bfloat16)
        kept = jnp.exp2((before - top) * factor)
        total = jnp.dot(weights, wide, preferred_element_type=jnp.float32)
        summed = total[:, :HEAD_DIM] + kept * part_sum[j, part, :HEAD_DIM]
        weight = total[:, HEAD_DIM:] + kept * part_sum[j, part, HEAD_DIM:]
        return top, summed, weight

    def middle_finish(j, step, heads, scores, wide):
        part = pl.ds(step * heads * rows, heads * rows)
        top, summed, weight = joined(j, part, scores, wide)
        part_sum[j, part, :HEAD_DIM] = summed
        part_sum[j, part, HEAD_DIM:] = weight
        part_top[j, part, :] = top

    def tail_finish(j, step, heads, scores, wide):
        part = pl.ds(step * heads * rows, heads * rows)
        _, summed, weight = joined(j, part, scores, wide)
        result = (summed / weight).astype(out_ref.dtype)
        for h, c in enumerate(columns(j, step, heads)):
            out_ref[:, c] = result[h * rows:(h + 1) * rows]

    def stage(kind, what):
        if kind == "near":
            from_plane(what, far - 1)
            from_side(what, far - 2)
        elif kind == "relay":
            from_side(what, far - 1)
            from_plane(what, far)
        elif kind == "last":
            from_side(what, far)
        elif kind == "main":
            for d in range(far):
                from_core(what, d)
            for d in range(far - 1):
                from_core_side(what, d)
            pipelined((what,), main_pieces, MAIN_HEADS, MAIN_AHEAD, main_finish)
        elif kind == "middle":
            from_core_side(what, far - 1)
            from_core(what, far)
            if level > 2:
                pipelined((what,), middle_pieces, MIDDLE_HEADS, MIDDLE_AHEAD, middle_finish)
        else:
            from_core_side(what, far)
            pipelined((what,), tail_pieces, TAIL_HEADS, TAIL_AHEAD, tail_finish)

    for j in range(KV_HEADS):
        own_copies[2 * j].wait()
        own_copies[2 * j + 1].wait()
        spread(0, j)

    for d in range(1, far + 1):
        @pl.when(z < d)
        def _():
            @pl.loop(0, KV_HEADS)
            def _(j):
                kv_buf[j, :, pl.ds(slot(d, 0) * rows, level * rows), :] = jnp.zeros(
                    (2, level * rows, HEAD_DIM), kv_buf.dtype
                )

    len_copy.wait()
    position = me * rows + lax.broadcasted_iota(jnp.int32, (1, rows), 1)
    start = jnp.zeros((1, rows), jnp.int32)
    end = jnp.int32(0)
    for k in range(len_buf.shape[0]):
        end = end + len_buf[k]
        start = jnp.where(end <= position, end, start)
    key_position = (me - reach) * rows + lax.broadcasted_iota(jnp.int32, bias.shape, 0)
    visible = (key_position >= start) & (key_position <= position)
    bias[...] = jnp.where(visible, 0.0, FILLER).astype(bias.dtype)

    for d in range(1, far - 1):
        for j in range(KV_HEADS):
            from_plane(j, d)
            from_side(j, d - 1)
    q_copy.wait()
    for kind, what in ORDER:
        stage(kind, what)

    for condition, *rest in sent:
        @pl.when(condition)
        def _():
            move(*rest).wait_send()


def solution(mesh):
    n = mesh.shape["ctx"]
    level = max(2, 8 // mesh.shape["groups"])

    def local(queries, keys, values, doc_lengths):
        rows = queries.shape[0]
        reach = n // 2
        slots = reach + level
        return pl.pallas_call(
            functools.partial(kernel, n, level),
            out_shape=jax.ShapeDtypeStruct(queries.shape, queries.dtype),
            in_specs=[pl.BlockSpec(memory_space=pltpu.HBM)] * 4,
            out_specs=pl.BlockSpec(memory_space=pltpu.VMEM),
            scratch_shapes=[
                pltpu.VMEM(queries.shape, queries.dtype),
                pltpu.VMEM((KV_HEADS, 2, slots * rows, HEAD_DIM), keys.dtype),
                pltpu.VMEM(((reach + 2) * rows, rows), keys.dtype),
                pltpu.SMEM(doc_lengths.shape, doc_lengths.dtype),
                pltpu.VMEM((KV_HEADS, GROUP * rows, 2 * HEAD_DIM), jnp.float32),
                pltpu.VMEM((KV_HEADS, GROUP * rows, HEAD_DIM), jnp.float32),
                pltpu.SemaphoreType.DMA((KV_HEADS, 2)),
                pltpu.SemaphoreType.DMA,
                pltpu.SemaphoreType.DMA,
                pltpu.SemaphoreType.DMA((KV_HEADS, slots, 3)),
                pltpu.SemaphoreType.DMA((KV_HEADS, slots)),
            ],
            compiler_params=pltpu.CompilerParams(collective_id=0, has_side_effects=True,
                                                 vmem_limit_bytes=min(60 << 20, (3 * n // 2 + 8) << 20)),
        )(*(
            pltpu.with_memory_space_constraint(x, pltpu.HBM)
            for x in (queries, keys, values, doc_lengths)
        ))

    spec = P(("groups", "ctx"), None)
    return jax.shard_map(
        local, mesh=mesh, in_specs=(spec, spec, spec, P("groups")), out_specs=spec, check_vma=False
    )
```

```python
import functools
import math

import jax
import jax.numpy as jnp
from jax import lax
from jax.experimental import pallas as pl
from jax.experimental.pallas import tpu as pltpu
from jax.sharding import PartitionSpec as P

HEADS = 32
KV_HEADS = 4
HEAD_DIM = 128
GROUP = HEADS // KV_HEADS
FILLER = -1e30
BY_PLANE = 2
MAIN_HEADS = 2
MAIN_AHEAD = 0
MIDDLE_HEADS = 2
MIDDLE_AHEAD = 0
TAIL_HEADS = 4
TAIL_AHEAD = 0
ORDER = (
    ("near", 0),
    ("near", 1),
    ("main", 0),
    ("near", 2),
    ("main", 1),
    ("near", 3),
    ("main", 2),
    ("relay", 0),
    ("main", 3),
    ("relay", 1),
    ("middle", 0),
    ("relay", 2),
    ("middle", 1),
    ("relay", 3),
    ("middle", 2),
    ("last", 0),
    ("middle", 3),
    ("last", 1),
    ("last", 2),
    ("tail", 0),
    ("last", 3),
    ("tail", 1),
    ("tail", 2),
    ("tail", 3),
)


def kernel(
    n, level, q_hbm, k_hbm, v_hbm, len_hbm, out_ref,
    q_buf, kv_buf, bias, len_buf, part_sum, part_top,
    own_sem, q_sem, len_sem, send_sem, recv_sem,
):
    rows = q_hbm.shape[0]
    reach = n // 2
    far = reach // level
    planes = n // level
    me = lax.axis_index("ctx")
    z, r = me // level, me % level
    core = r + 1 - 2 * (r % 2)
    side = (r + 2) % level
    side_core = core + side - r

    def slot(d, lane):
        return (far - d) * level + lane

    def part(j, s):
        return kv_buf.at[j, :, pl.ds(pl.multiple_of(s * rows, rows), rows), :]

    def move(j, s, s_there, kind, device):
        return pltpu.make_async_remote_copy(
            src_ref=part(j, s), dst_ref=part(j, s_there),
            send_sem=send_sem.at[j, s, kind], recv_sem=recv_sem.at[j, s_there],
            device_id={"ctx": device}, device_id_type=pl.DeviceIdType.MESH,
        )

    def need(d, source, target):
        distance = d * level + target - source
        return (distance >= 0) & (distance <= reach)

    def there(d):
        return z >= d

    sent = []

    def send(condition, j, s, s_there, kind, device):
        @pl.when(condition)
        def _():
            move(j, s, s_there, kind, device).start()

        sent.append((condition, j, s, s_there, kind, device))

    def arrived(condition, j, s):
        @pl.when(condition)
        def _():
            move(j, s, s, 0, me - r + core).wait_recv()

    barrier = pltpu.get_barrier_semaphore()

    def greet(device):
        pl.semaphore_signal(
            barrier, inc=1, device_id={"ctx": device}, device_id_type=pl.DeviceIdType.MESH
        )

    greet(me - r + core)
    if level > 2:
        greet(me - r + side)

    @pl.when(z > 0)
    def _():
        greet(me - level)

    @pl.when(z < planes - 1)
    def _():
        greet(me + level)

    own = slot(0, r)
    own_copies = []
    for j in range(KV_HEADS):
        for t, ref in enumerate((k_hbm, v_hbm)):
            own_copies.append(pltpu.make_async_copy(
                ref.at[:, pl.ds(j * HEAD_DIM, HEAD_DIM)],
                kv_buf.at[j, t, pl.ds(pl.multiple_of(own * rows, rows), rows), :],
                own_sem.at[j, t],
            ))
            own_copies[-1].start()
    q_copy = pltpu.make_async_copy(q_hbm, q_buf, q_sem)
    q_copy.start()
    len_copy = pltpu.make_async_copy(len_hbm, len_buf, len_sem)
    len_copy.start()

    pl.semaphore_wait(
        barrier,
        (2 if level > 2 else 1) + (z > 0).astype(jnp.int32) + (z < planes - 1).astype(jnp.int32),
    )

    def by_plane(j):
        return level > 2 and j >= KV_HEADS - BY_PLANE

    def spread(d, j):
        s = slot(d, r)
        if d < far:
            send(there(d) & (z < planes - 1), j, s, slot(d + 1, r), 0, me + level)
        if level > 2 and not (d == far and by_plane(j)):
            send(
                there(d) & (need(d, r, side) | need(d, r, side_core)),
                j, s, s, 1, me - r + side,
            )
        send(there(d) & need(d, r, core), j, s, s, 2, me - r + core)

    def from_plane(j, d):
        arrived(there(d), j, slot(d, r))
        spread(d, j)

    def from_side(j, d):
        if level > 2:
            s = slot(d, side)
            wanted = there(d) & (need(d, side, r) | need(d, side, core))
            if by_plane(j) and d == far:
                wanted = there(d) & (r < level // 2)
            arrived(wanted, j, s)
            if by_plane(j) and d == far - 1:
                climbs = there(d) & (r < level // 2) & (z < planes - 1)
                send(climbs, j, s, slot(far, side), 0, me + level)
            send(there(d) & need(d, side, core), j, s, s, 2, me - r + core)

    def from_core(j, d):
        arrived(there(d) & need(d, core, r), j, slot(d, core))

    def from_core_side(j, d):
        if level > 2:
            arrived(there(d) & need(d, side_core, r), j, slot(d, side_core))

    unit = (
        lax.broadcasted_iota(jnp.int32, (rows, rows), 0)
        == lax.broadcasted_iota(jnp.int32, (rows, rows), 1)
    ).astype(bias.dtype)
    factor = math.log2(math.e) / math.sqrt(HEAD_DIM)

    def blocks(pieces):
        return [pl.ds(pl.multiple_of(first * rows, rows), count * rows) for first, count in pieces]

    if level > 2:
        upper = r // 2
        third = (r == 2).astype(jnp.int32)
        first = (r == 0).astype(jnp.int32)
        main_pieces = [
            (4 + upper * (r + 1), 4 + upper * (r + 1) - r, 2),
            (8 + upper * (r - 1), 8 + upper * (r - 1) - r, 1),
            (8 + r, 8 + first, 1),
        ]
        middle_pieces = [
            (r + 2 * upper, 2 * upper, 1),
            (7 - third - 6 * first, 9 - 8 * first, 1),
            (6 - third, 6 - third - r, 2),
        ]
        tail_pieces = [(2 + r // 3, 2 + r // 3 - r, 2)]
    else:
        main_pieces = [(r + level, level, reach + 1 - level)]
        tail_pieces = [(r, 0, level)]

    def operands(j, pieces):
        places = blocks([(place, count) for place, _, count in pieces])
        keys = jnp.concatenate([kv_buf[j, 0, p, :] for p in places], axis=0)
        mask = jnp.concatenate(
            [bias[p, :] for p in blocks([(distance, count) for _, distance, count in pieces])], axis=0
        )
        value_block = jnp.concatenate([kv_buf[j, 1, p, :] for p in places], axis=0)
        wide = jnp.concatenate([value_block, jnp.ones_like(value_block)], axis=1)
        return jnp.concatenate([keys, mask], axis=1), wide

    def columns(j, step, heads):
        first = j * GROUP + step * heads
        return [pl.ds((first + h) * HEAD_DIM, HEAD_DIM) for h in range(heads)]

    def pipelined(chosen, pieces, heads, ahead, finish):
        tasks = [(j, step) for j in chosen for step in range(GROUP // heads)]
        queue = []

        def begin(j, step):
            block = jnp.concatenate(
                [jnp.concatenate([q_buf[:, c], unit], axis=1) for c in columns(j, step, heads)],
                axis=0,
            )
            key_block, wide = operands(j, pieces)
            queue.append((lax.dot_general(
                block, key_block, (((1,), (1,)), ((), ())), preferred_element_type=jnp.float32
            ), wide))

        for task in tasks[:ahead]:
            begin(*task)
        for i, (j, step) in enumerate(tasks):
            if i + ahead < len(tasks):
                begin(*tasks[i + ahead])
            finish(j, step, heads, *queue.pop(0))

    def main_finish(j, step, heads, scores, wide):
        part = pl.ds(step * heads * rows, heads * rows)
        top = jnp.max(scores, axis=1, keepdims=True)
        weights = jnp.exp2((scores - top) * factor).astype(jnp.bfloat16)
        part_sum[j, part, :] = jnp.dot(weights, wide, preferred_element_type=jnp.float32)
        part_top[j, part, :] = jnp.broadcast_to(top, (heads * rows, HEAD_DIM))

    def joined(j, part, scores, wide):
        before = part_top[j, part, :]
        top = jnp.maximum(before, jnp.max(scores, axis=1, keepdims=True))
        spread_top = jnp.concatenate([top] * (scores.shape[1] // HEAD_DIM), axis=1)
        weights = jnp.exp2((scores - spread_top) * factor).astype(jnp.bfloat16)
        kept = jnp.exp2((before - top) * factor)
        total = jnp.dot(weights, wide, preferred_element_type=jnp.float32)
        summed = total[:, :HEAD_DIM] + kept * part_sum[j, part, :HEAD_DIM]
        weight = total[:, HEAD_DIM:] + kept * part_sum[j, part, HEAD_DIM:]
        return top, summed, weight

    def middle_finish(j, step, heads, scores, wide):
        part = pl.ds(step * heads * rows, heads * rows)
        top, summed, weight = joined(j, part, scores, wide)
        part_sum[j, part, :HEAD_DIM] = summed
        part_sum[j, part, HEAD_DIM:] = weight
        part_top[j, part, :] = top

    def tail_finish(j, step, heads, scores, wide):
        part = pl.ds(step * heads * rows, heads * rows)
        _, summed, weight = joined(j, part, scores, wide)
        result = (summed / weight).astype(out_ref.dtype)
        for h, c in enumerate(columns(j, step, heads)):
            out_ref[:, c] = result[h * rows:(h + 1) * rows]

    def stage(kind, what):
        if kind == "near":
            from_plane(what, far - 1)
            from_side(what, far - 2)
        elif kind == "relay":
            from_side(what, far - 1)
            from_plane(what, far)
        elif kind == "last":
            from_side(what, far)
        elif kind == "main":
            for d in range(far):
                from_core(what, d)
            for d in range(far - 1):
                from_core_side(what, d)
            pipelined((what,), main_pieces, MAIN_HEADS, MAIN_AHEAD, main_finish)
        elif kind == "middle":
            from_core_side(what, far - 1)
            from_core(what, far)
            if level > 2:
                pipelined((what,), middle_pieces, MIDDLE_HEADS, MIDDLE_AHEAD, middle_finish)
        else:
            from_core_side(what, far)
            pipelined((what,), tail_pieces, TAIL_HEADS, TAIL_AHEAD, tail_finish)

    for j in range(KV_HEADS):
        own_copies[2 * j].wait()
        own_copies[2 * j + 1].wait()
        spread(0, j)

    for d in range(1, far + 1):
        @pl.when(z < d)
        def _():
            @pl.loop(0, KV_HEADS)
            def _(j):
                kv_buf[j, :, pl.ds(slot(d, 0) * rows, level * rows), :] = jnp.zeros(
                    (2, level * rows, HEAD_DIM), kv_buf.dtype
                )

    len_copy.wait()
    position = me * rows + lax.broadcasted_iota(jnp.int32, (1, rows), 1)
    start = jnp.zeros((1, rows), jnp.int32)
    end = jnp.int32(0)
    for k in range(len_buf.shape[0]):
        end = end + len_buf[k]
        start = jnp.where(end <= position, end, start)
    key_position = (me - reach) * rows + lax.broadcasted_iota(jnp.int32, bias.shape, 0)
    visible = (key_position >= start) & (key_position <= position)
    bias[...] = jnp.where(visible, 0.0, FILLER).astype(bias.dtype)

    for d in range(1, far - 1):
        for j in range(KV_HEADS):
            from_plane(j, d)
            from_side(j, d - 1)
    q_copy.wait()
    for kind, what in ORDER:
        stage(kind, what)

    for condition, *rest in sent:
        @pl.when(condition)
        def _():
            move(*rest).wait_send()


def solution(mesh):
    n = mesh.shape["ctx"]
    level = max(2, 8 // mesh.shape["groups"])

    def local(queries, keys, values, doc_lengths):
        rows = queries.shape[0]
        reach = n // 2
        slots = reach + level
        return pl.pallas_call(
            functools.partial(kernel, n, level),
            out_shape=jax.ShapeDtypeStruct(queries.shape, queries.dtype),
            in_specs=[pl.BlockSpec(memory_space=pltpu.HBM)] * 4,
            out_specs=pl.BlockSpec(memory_space=pltpu.VMEM),
            scratch_shapes=[
                pltpu.VMEM(queries.shape, queries.dtype),
                pltpu.VMEM((KV_HEADS, 2, slots * rows, HEAD_DIM), keys.dtype),
                pltpu.VMEM(((reach + 2) * rows, rows), keys.dtype),
                pltpu.SMEM(doc_lengths.shape, doc_lengths.dtype),
                pltpu.VMEM((KV_HEADS, GROUP * rows, 2 * HEAD_DIM), jnp.float32),
                pltpu.VMEM((KV_HEADS, GROUP * rows, HEAD_DIM), jnp.float32),
                pltpu.SemaphoreType.DMA((KV_HEADS, 2)),
                pltpu.SemaphoreType.DMA,
                pltpu.SemaphoreType.DMA,
                pltpu.SemaphoreType.DMA((KV_HEADS, slots, 3)),
                pltpu.SemaphoreType.DMA((KV_HEADS, slots)),
            ],
            compiler_params=pltpu.CompilerParams(collective_id=0, has_side_effects=True,
                                                 vmem_limit_bytes=min(60 << 20, (3 * n // 2 + 8) << 20)),
        )(*(
            pltpu.with_memory_space_constraint(x, pltpu.HBM)
            for x in (queries, keys, values, doc_lengths)
        ))

    spec = P(("groups", "ctx"), None)
    return jax.shard_map(
        local, mesh=mesh, in_specs=(spec, spec, spec, P("groups")), out_specs=spec, check_vma=False
    )
```
